32 devices in a mesh: sec: 2 (over core), sp: 4 (over y, x), dev: 4 (over z).
Axes of the slice: x: 2, y: 2, z: 4, core: 2. Of those that a mesh axis runs over, the one named last changes fastest.
Arguments:
- patch_qkv: bfloat16 [4096, 3, 1280], P(('sec', 'sp', 'dev')), may hold values from -13 to 13
- patch_state: bfloat16 [4096, 1280], P(('sec', 'sp', 'dev')), may hold values from -6 to 6
- window_index: int32 [32, 128], P(('sec', 'sp', 'dev')), may hold values from 0 to 127, each once within a row
- patch_owner: int32 [4096, 1], P(('sec', 'sp', 'dev')), may hold values from 0 to 7; in each aligned block of 128 rows (0 to 127, 128 to 255, ...) at most 32 rows name the same one
- source_request: int32 [8, 8], P(('sec', 'dev')), may hold values from 0 to 3, never falling along the last dimension, each value on 1 to 4 neighbouring positions
- norm_gain: float32 [1280], replicated, may hold values from 0.1 to 1.9
- w_qkv: bfloat16 [1280, 3, 1280], P(None, None, 'sp'), may hold values from -0.15625 to 0.15625
- b_qkv: bfloat16 [3, 1280], P(None, 'sp'), may hold values from -12 to 12
Outputs:
- out_rows: bfloat16 [4096, 1280], P(('sec', 'sp', 'dev'))
The draws below stay inside these ranges and needn't reach their ends.
Inputs may be any that keep to these rules, and one draw needn't show every extreme that they name: `window_index`: each row is a permutation of the 128 local patch indices of one device. `patch_owner`: among the 128 patches of one device no owner is named more than 32 times, and on some device one owner is named exactly 32 times. `source_request`: along each row the request number never falls; each request covers 1 to 4 consecutive source positions, one exactly 4.
All inputs are finite; a program needn't handle non-finite values.
Results may differ from the reference program's by a relative error of at most 0.012.
The reference program's roundings to bfloat16 on the way (of `window_out`, `moved`, `group_rows`, `normed`, `projected`, `weights` and `mixed`) count: a program that leaves them out, or rounds other values in their place, can miss the bound.
Values may be sent and summed in bfloat16 or wider, within the bound.
No kernel may reach another device: no remote copies, remote signals or barrier semaphores. Data moves between devices by JAX's collectives and lax.ppermute only.
A program may use at most 64 MiB of HBM per device.

```python
import math
import jax
import jax.numpy as jnp
import numpy as np
from jax import lax

HV = 1280
HEADS = 16
HD = 80
WIN = 64
P_DEV = 128
OWNERS = 8
CAP = 32
REQS = 4
RMOST = 4
PATCHES = 4096
N_SEC = 2
N_SP = 4
N_DEV = 4


def draw_patch_qkv(key, part):
    noise_key = jax.random.fold_in(key, 0)
    values = jax.random.truncated_normal(noise_key, -6.0, 6.0, (PATCHES, 3, HV), jnp.float32)
    return values.astype(jnp.bfloat16)


def draw_b_qkv(key, part):
    noise_key = jax.random.fold_in(key, 0)
    values = 0.3 * jax.random.truncated_normal(noise_key, -6.5, 6.5, (3, HV), jnp.float32)
    return values.astype(jnp.bfloat16)


def level_of(own_key, dims, pieces, smallest, top_value):
    loudness, own = 1.0, jax.random.fold_in(own_key, 6)
    for position, blocks in pieces:
        steps = jnp.exp(jax.random.uniform(jax.random.fold_in(own, position), (blocks,), jnp.float32, smallest / len(pieces), top_value / len(pieces)))
        loudness = loudness * jnp.repeat(steps, dims[position] // blocks).reshape([-1 if axis == position else 1 for axis in range(len(dims))])
    return loudness


def split_up(amount, total, limit, skew):
    loads = [(1 << 20) // math.isqrt(rank ** skew) + 1 for rank in range(2, amount + 1)]
    surplus, counts = total - limit - (amount - 1), [1] * (amount - 1)
    while surplus > 0:
        free = [i for i in range(amount - 1) if counts[i] < limit]
        mass, remaining = sum([loads[i] for i in free]), surplus
        for i in free:
            more = min(limit - counts[i], max(1, remaining * loads[i] // mass), surplus)
            counts[i] = counts[i] + more
            surplus = surplus - more
    return np.array([limit] + counts)


def ragged_sizes(own_key, amount, total, most, slope):
    if amount == 2:
        one = jax.random.randint(own_key, (), max(1, total - most), min(most, total - 1) + 1)
        return jnp.stack([one, total - one])
    lengths = jnp.asarray(split_up(amount, total, most, slope), jnp.int32)
    twos = (amount - 1) // 2
    giver, taker = lengths[1:1 + 2 * twos:2], lengths[2:2 + 2 * twos:2]
    room = jnp.minimum(giver - 1, most - taker)
    passed = jax.random.randint(jax.random.fold_in(own_key, 1), (twos,), 0, 1 << 20) % (room + 1)
    lengths = lengths.at[1:1 + 2 * twos:2].set(giver - passed).at[2:2 + 2 * twos:2].set(taker + passed)
    return lengths[jax.random.permutation(jax.random.fold_in(own_key, 2), amount)]


def shared_out(key, own, number, rows, amount, top, reach, lean):
    sequence = jax.random.permutation(key, amount)
    packed, common = portions_of(amount, rows * top, reach, lean, True), portions_of(amount, rows * top, reach, lean, False)
    places = jnp.arange(amount)

    def named(tallies, offset_by):
        used = int((tallies > 0).sum())
        fixed = max(1, used // 4)
        moved = fixed + (places - fixed + offset_by * (used - fixed)) % max(1, amount - fixed)
        return jnp.zeros((amount,), jnp.int32).at[sequence[jnp.where(places < fixed, places, moved)]].set(jnp.asarray(tallies, jnp.int32))

    tallies = jnp.where(number % 4 == 0, named(packed, number // 4), named(common, number - number // 4 - 1))
    mixed = jax.random.permutation(jax.random.fold_in(own, 3), amount)
    source_of, sink = mixed[0:amount // 2 * 2:2], mixed[1:amount // 2 * 2:2]
    slack = jnp.minimum(tallies[source_of] - 1, reach - tallies[sink]) // 2
    slack = jnp.where((source_of == sequence[0]) | (sink == sequence[0]) | (tallies[sink] == 0), 0, jnp.maximum(slack, 0))
    moved = jax.random.randint(jax.random.fold_in(own, 4), (amount // 2,), 0, 1 << 20) % (slack + 1)
    tallies = tallies.at[source_of].add(-moved).at[sink].add(moved)
    labels = jnp.searchsorted(jnp.cumsum(tallies), jnp.arange(rows * top), side="right").astype(jnp.int32)
    grid = labels.reshape(top, rows).T
    grid = grid[jax.random.permutation(jax.random.fold_in(own, 1), rows)]
    offset_by = jax.random.randint(jax.random.fold_in(own, 2), (rows, 1), 0, top)
    return jnp.take_along_axis(grid, (jnp.arange(top)[None, :] + offset_by) % top, axis=1)


def portions_of(amount, total, bound, slope, full):
    portions = [(1 << 20) // math.isqrt(grade ** slope) + 1 for grade in range(1, amount + 1)]
    largest = bound if full else min(bound, max(-(-total // amount), total * portions[0] // sum(portions)))
    least = 1 if total - largest >= amount - 1 else 0
    holding, rest = [largest] + [least] * (amount - 1), total - largest - least * (amount - 1)
    while rest > 0:
        movable = [i for i in range(1, amount) if holding[i] < largest] or [i for i in range(1, amount) if holding[i] < bound]
        mass, remaining = sum([portions[i] for i in movable]), rest
        for i in movable:
            addition = min(bound - holding[i], max(1, remaining * portions[i] // mass), rest)
            holding[i] = holding[i] + addition
            rest = rest - addition
    return np.array(holding)


def gaussian(own_key, dims, spread, bound, cuts=(), held_as=jnp.bfloat16):
    entries = spread * jax.random.normal(own_key, dims, jnp.float32)
    if cuts:
        entries = entries * level_of(own_key, dims, cuts, -0.22, 0.18)
    return jnp.clip(entries, -bound, bound).astype(held_as)


def setup_inputs(seed: int = 0) -> dict:
    streams_of = jax.random.split(jax.random.key(seed), 9)
    patch_qkv = draw_patch_qkv(jax.random.fold_in(streams_of[8], 71), 0)
    patch_state = gaussian(streams_of[1], (PATCHES, HV), 1.0, 6.0, ((0, 32),))
    window_index = jax.vmap(lambda own: jax.random.permutation(own, P_DEV))(jax.random.split(streams_of[2], (N_SEC * N_SP * N_DEV))).reshape((N_SEC * N_SP * N_DEV, P_DEV)).astype(jnp.int32)
    patch_owner_keys = jax.random.split(jax.random.fold_in(streams_of[3], 1), PATCHES // P_DEV)
    patch_owner_turns = jax.random.permutation(jax.random.fold_in(streams_of[3], 3), PATCHES // P_DEV)
    patch_owner = jax.vmap(lambda own, number: shared_out(jax.random.fold_in(streams_of[3], 2), own, number, P_DEV, OWNERS, 1, CAP, 2))(patch_owner_keys, patch_owner_turns).reshape((PATCHES, 1))
    source_request = jax.vmap(lambda own: jnp.searchsorted(jnp.cumsum(ragged_sizes(own, REQS, OWNERS, RMOST, 2)), jnp.arange(OWNERS), side="right"))(jax.random.split(streams_of[4], OWNERS)).reshape((OWNERS, OWNERS)).astype(jnp.int32)
    norm_gain = jnp.clip(1.0 + 0.18 * jax.random.normal(streams_of[5], (HV,), jnp.float32), 0.1, 1.9)
    w_qkv = gaussian(streams_of[6], (HV, 3, HV), HV ** -0.5, 0.15625, ((2, 4),))
    b_qkv = draw_b_qkv(jax.random.fold_in(streams_of[8], 71), 0)
    return dict(patch_qkv=patch_qkv, patch_state=patch_state, window_index=window_index, patch_owner=patch_owner, source_request=source_request, norm_gain=norm_gain, w_qkv=w_qkv, b_qkv=b_qkv)


NORM_EPS = 1e-06

def normalize(rows_in, gain_row):
    rows_in = rows_in.astype(jnp.float32)
    mean_sq = lax.optimization_barrier(jnp.mean(rows_in * rows_in, axis=-1, keepdims=True))
    return (rows_in * lax.rsqrt(mean_sq + NORM_EPS) * gain_row).astype(jnp.bfloat16)

def softmax_rows(scores):
    row_max = lax.optimization_barrier(jnp.max(scores, axis=-1, keepdims=True))
    expo_vals = jnp.exp(scores - row_max)
    return (expo_vals / lax.optimization_barrier(jnp.sum(expo_vals, axis=-1, keepdims=True))).astype(jnp.bfloat16)

def window_attend(qkv_rows, order_ids, head_count, head_size, window_span):
    num_rows = qkv_rows.shape[0]
    row_width = head_count * head_size
    ordered = jnp.take(qkv_rows, order_ids, axis=0).astype(jnp.float32)
    ordered = ordered.reshape(num_rows // window_span, window_span, 3, head_count, head_size)
    scores = jnp.einsum('wqhd,wkhd->whqk', ordered[:, :, 0], ordered[:, :, 1]) * head_size ** (-0.5)
    weights = softmax_rows(scores)
    weights = lax.optimization_barrier(weights).astype(jnp.float32)
    mixed = jnp.einsum('whqk,wkhd->wqhd', weights, ordered[:, :, 2])
    mixed = mixed.reshape(num_rows, row_width).astype(jnp.bfloat16)
    return jnp.zeros((num_rows, row_width), jnp.bfloat16).at[order_ids].set(mixed)

def owner_attend(group_rows, live_slots, request, gain_row, w_all, b_all, head_count, head_size):
    group_size = group_rows.shape[0]
    normed = normalize(group_rows, gain_row)
    projected = jnp.dot(normed, w_all.reshape(w_all.shape[0], -1), preferred_element_type=jnp.float32)
    projected = projected.reshape(group_size, 3, -1) + b_all.astype(jnp.float32)
    projected = lax.optimization_barrier(projected.astype(jnp.bfloat16)).astype(jnp.float32)
    projected = projected.reshape(group_size, 3, head_count, head_size)
    scores = jnp.einsum('qhd,khd->hqk', projected[:, 0], projected[:, 1])
    allowed = (request[:, None] == request[None, :]) & (live_slots[None, :] > 0)
    scores = jnp.where(allowed[None], scores * head_size ** (-0.5), -1e+30)
    weights = lax.optimization_barrier(softmax_rows(scores)).astype(jnp.float32)
    mixed = jnp.einsum('hqk,khd->qhd', weights, projected[:, 2])
    return mixed.reshape(group_size, head_count * head_size).astype(jnp.bfloat16)

def reference(patch_qkv, patch_state, window_index, patch_owner, source_request, norm_gain, w_qkv, b_qkv):
    devices = N_SEC * N_SP * N_DEV
    owners = N_SEC * N_DEV
    qkv_dev = patch_qkv.reshape(devices, P_DEV, 3, HV)
    window_out = lax.map(lambda key_item: window_attend(key_item[0], key_item[1], HEADS, HD, WIN), (qkv_dev, window_index))
    window_out = lax.optimization_barrier(window_out)
    state_rows = patch_state.reshape(devices, P_DEV, HV)
    moved = (state_rows.astype(jnp.float32) + window_out.astype(jnp.float32)).astype(jnp.bfloat16)
    owner_id = patch_owner.reshape(devices, P_DEV).astype(jnp.int32)
    owner_hits = (owner_id[:, :, None] == jnp.arange(owners, dtype=jnp.int32)[None, None, :]).astype(jnp.int32)
    slot_rank = lax.optimization_barrier(jnp.sum((jnp.cumsum(owner_hits, axis=1) - 1) * owner_hits, axis=2)).astype(jnp.int32)
    slot_id = (owner_id * CAP + slot_rank).astype(jnp.int32)
    row_ids = jnp.arange(devices, dtype=jnp.int32)[:, None]
    buffer = jnp.zeros((devices, owners * CAP, HV), jnp.bfloat16).at[row_ids, slot_id].set(moved)
    live_slots = jnp.zeros((devices, owners * CAP), jnp.int32).at[row_ids, slot_id].set(1)
    grouped = buffer.reshape(N_SEC, N_SP, N_DEV, owners, CAP, HV).transpose(3, 0, 2, 1, 4, 5).reshape(owners, -1, HV)
    live_group = live_slots.reshape(N_SEC, N_SP, N_DEV, owners, CAP).transpose(3, 0, 2, 1, 4).reshape(owners, -1)
    request = jnp.repeat(source_request, N_SP * CAP, axis=1)
    mixed = lax.map(lambda key_item: owner_attend(key_item[0], key_item[1], key_item[2], norm_gain, w_qkv, b_qkv, HEADS, HD), (grouped, live_group, request))
    back_rows = mixed.reshape(owners, N_SEC, N_DEV, N_SP, CAP, HV).transpose(1, 3, 2, 0, 4, 5).reshape(devices, owners * CAP, HV)
    gathered = jnp.take_along_axis(back_rows, slot_id[:, :, None], axis=1)
    result = (moved.astype(jnp.float32) + gathered.astype(jnp.float32)).astype(jnp.bfloat16)
    return result.reshape(devices * P_DEV, HV)
```

```python
import functools

import jax
import jax.numpy as jnp
from jax import lax
from jax.experimental import pallas as pl
from jax.experimental.pallas import tpu as pltpu
from jax.sharding import PartitionSpec as P

HD = 80
WIN = 64
NORM_EPS = 1e-06
NEG = -1e30
EMPTY = 2.0**60
LANES = 128


def normalize(rows_in, gain_row):
    rows_in = rows_in.astype(jnp.float32)
    mean_sq = jnp.mean(rows_in * rows_in, axis=-1, keepdims=True)
    return (rows_in * lax.rsqrt(mean_sq + NORM_EPS) * gain_row).astype(jnp.bfloat16)


def softmax_rows(scores):
    row_max = jnp.max(scores, axis=-1, keepdims=True)
    expo_vals = jnp.exp(scores - row_max)
    return (expo_vals / jnp.sum(expo_vals, axis=-1, keepdims=True)).astype(jnp.bfloat16)


def window_attend(qkv_rows, order_ids, head_size, window_span):
    num_rows = qkv_rows.shape[0]
    row_width = qkv_rows.shape[2]
    head_count = row_width // head_size
    ordered = jnp.take(qkv_rows, order_ids, axis=0)
    ordered = ordered.reshape(num_rows // window_span, window_span, 3, head_count, head_size)
    scores = jnp.einsum(
        "wqhd,wkhd->whqk", ordered[:, :, 0], ordered[:, :, 1], preferred_element_type=jnp.float32
    ) * head_size ** (-0.5)
    weights = softmax_rows(scores)
    mixed = jnp.einsum(
        "whqk,wkhd->wqhd", weights, ordered[:, :, 2], preferred_element_type=jnp.float32
    )
    mixed = mixed.reshape(num_rows, row_width).astype(jnp.bfloat16)
    return jnp.zeros((num_rows, row_width), jnp.bfloat16).at[order_ids].set(mixed)


def owner_attend(query, keys_all, values_all, request, live_keys, head_size):
    group_size, head_count, _ = query.shape
    q_block = 512
    scale = head_size ** (-0.5)
    open_keys = live_keys > 0

    def one_block(block_start):
        rows_q = lax.dynamic_slice_in_dim(query, block_start, q_block, 0)
        reqs_q = lax.dynamic_slice_in_dim(request, block_start, q_block, 0)
        scores = jnp.einsum("qhd,khd->hqk", rows_q, keys_all, preferred_element_type=jnp.float32)
        allowed = (reqs_q[:, None] == request[None, :]) & open_keys[None, :]
        scores = jnp.where(allowed[None], scores * scale, NEG)
        weights = softmax_rows(scores)
        mixed = jnp.einsum("hqk,khd->qhd", weights, values_all, preferred_element_type=jnp.float32)
        return mixed.astype(jnp.bfloat16)

    starts = jnp.arange(group_size // q_block, dtype=jnp.int32) * q_block
    blocks = lax.map(one_block, starts)
    return blocks.reshape(group_size, head_count * head_size)


def shards_general(
    patch_qkv, patch_state, window_index, patch_owner, source_request, norm_gain, w_qkv, b_qkv
):
    num_rows = patch_qkv.shape[0]
    row_width = patch_qkv.shape[2]
    sections = lax.axis_size("sec")
    groups = lax.axis_size("sp")
    members = lax.axis_size("dev")
    owners = sections * members
    capacity = max(2, 2 * num_rows // owners)
    local_width = w_qkv.shape[2]
    local_heads = local_width // HD
    window_out = lax.optimization_barrier(window_attend(patch_qkv, window_index[0], HD, WIN))
    moved = (patch_state.astype(jnp.float32) + window_out.astype(jnp.float32)).astype(jnp.bfloat16)
    owner_id = patch_owner[:, 0]
    owner_hits = (owner_id[:, None] == jnp.arange(owners, dtype=jnp.int32)[None, :]).astype(
        jnp.int32
    )
    slot_rank = jnp.sum((jnp.cumsum(owner_hits, axis=0) - 1) * owner_hits, axis=1)
    slot_id = owner_id * capacity + slot_rank
    picker = (jnp.arange(owners * capacity, dtype=jnp.int32)[:, None] == slot_id[None, :]).astype(
        jnp.bfloat16
    )
    outgoing = jnp.dot(picker, moved, preferred_element_type=jnp.float32).astype(jnp.bfloat16)
    outgoing = outgoing.reshape(owners, capacity, row_width)
    filled = jnp.max(picker, axis=1).reshape(owners, capacity)
    incoming, arrived = (
        lax.all_to_all(outgoing, ("sec", "dev"), split_axis=0, concat_axis=0, tiled=True),
        lax.all_to_all(filled, ("sec", "dev"), split_axis=0, concat_axis=0, tiled=True),
    )
    group_size = owners * groups * capacity
    rows_all, live_all = (
        lax.all_gather(incoming, "sp", axis=1, tiled=True),
        lax.all_gather(arrived, "sp", axis=1, tiled=True),
    )
    normed = normalize(rows_all.reshape(group_size, row_width), norm_gain)
    projected = jnp.einsum("gf,fch->gch", normed, w_qkv, preferred_element_type=jnp.float32)
    projected = (projected + b_qkv.astype(jnp.float32)).astype(jnp.bfloat16)
    query = projected[:, 0].reshape(group_size, local_heads, HD)
    keys_all = projected[:, 1].reshape(group_size, local_heads, HD)
    values_all = projected[:, 2].reshape(group_size, local_heads, HD)
    request = jnp.repeat(source_request[0], groups * capacity)
    live_keys = live_all.reshape(group_size)
    mixed = owner_attend(query, keys_all, values_all, request, live_keys, HD)
    pieces = mixed.reshape(owners, groups, capacity, local_width)
    returned = lax.all_to_all(pieces, "sp", split_axis=1, concat_axis=3, tiled=True).reshape(
        owners, capacity, row_width
    )
    result = lax.all_to_all(returned, ("sec", "dev"), split_axis=0, concat_axis=0, tiled=True)
    result = result.reshape(owners * capacity, row_width)
    back_rows = jnp.einsum("sp,sw->pw", picker, result, preferred_element_type=jnp.float32)
    return (moved.astype(jnp.float32) + back_rows).astype(jnp.bfloat16)


SEC, LINES, PLANES = 2, 4, 4
BLOCKS = SEC * PLANES
LINE_ORDER = ((0, 1, 2, 3), (0, 2, 1, 3))


def dot_t(a, b):
    return lax.dot_general(a, b, (((1,), (1,)), ((), ())), preferred_element_type=jnp.float32)


def dot_n(a, b):
    return lax.dot_general(a, b, (((1,), (0,)), ((), ())), preferred_element_type=jnp.float32)


def iota(shape, dim):
    return lax.broadcasted_iota(jnp.int32, shape, dim)


def tiles_of(head):
    first, last = head * HD // LANES, (head * HD + HD - 1) // LANES
    return first, last + 1


def head_mask(head):
    first, end = tiles_of(head)
    lane = iota((1, (end - first) * LANES), 1) + first * LANES
    return (lane >= head * HD) & (lane < head * HD + HD)


def window_kernel(pos_ref, qkv_ref, state_ref, order_ref, owner_ref, moved_ref, lo_ref, hi_ref, *out_refs):
    rows, width = state_ref.shape
    heads = width // HD
    cap = out_refs[0].shape[0]
    dev, sec = pos_ref[0], pos_ref[1]
    square = (rows, rows)
    sub, lane = iota(square, 0), iota(square, 1)

    hit = (jnp.broadcast_to(order_ref[...], square) == sub) & (lane < WIN)
    in_first = jnp.sum(hit.astype(jnp.float32), axis=1, keepdims=True)
    in_first = jnp.broadcast_to(in_first, square)
    bias = jnp.where(in_first == in_first.T, 0.0, NEG)

    tile = [None] * (width // LANES)
    for head in range(heads):
        first, end = tiles_of(head)
        cols = slice(first * LANES, end * LANES)
        mask = head_mask(head)
        query = jnp.where(mask, qkv_ref[0, :, cols], jnp.zeros((), jnp.bfloat16))
        scores = dot_t(query, qkv_ref[1, :, cols]) * HD ** (-0.5) + bias
        expo = jnp.exp(scores - jnp.max(scores, axis=1, keepdims=True))
        weights = expo * (1.0 / jnp.sum(expo, axis=1, keepdims=True))
        mixed = dot_n(weights.astype(jnp.bfloat16), qkv_ref[2, :, cols])
        for t in range(first, end):
            part = slice((t - first) * LANES, (t - first + 1) * LANES)
            if tile[t] is None:
                tile[t] = mixed[:, part]
            else:
                tile[t] = jnp.where(mask[:, part], mixed[:, part], tile[t])
    for t in range(width // LANES):
        cols = slice(t * LANES, (t + 1) * LANES)
        window_out = tile[t].astype(jnp.bfloat16).astype(jnp.float32)
        moved_ref[:, cols] = (state_ref[:, cols].astype(jnp.float32) + window_out).astype(jnp.bfloat16)

    owner_row = jnp.broadcast_to(owner_ref[...], square).astype(jnp.float32)
    owner_col = owner_row.T
    same = owner_row == owner_col

    def relative(owner):
        owner = owner.astype(jnp.int32)
        return ((owner & (PLANES - 1)) ^ dev) * SEC + ((owner // PLANES) ^ sec)

    rank_row = jnp.sum((same & (sub < lane)).astype(jnp.float32), axis=0, keepdims=True)
    slot_row = relative(owner_row[:1]) * cap + rank_row.astype(jnp.int32)
    picker = iota((BLOCKS * cap, rows), 0) == jnp.broadcast_to(slot_row, (BLOCKS * cap, rows))
    filled = jnp.sum(picker.astype(jnp.float32), axis=1, keepdims=True)
    mark = jnp.where((filled == 0.0) & (iota((BLOCKS * cap, LANES), 1) == 0), EMPTY, 0.0)
    picked = dot_n(picker.astype(jnp.bfloat16), moved_ref[...])
    for b in range(BLOCKS):
        span = slice(b * cap, (b + 1) * cap)
        out_refs[b][:, :LANES] = (picked[span, :LANES] + mark[span]).astype(jnp.bfloat16)
        out_refs[b][:, LANES:] = picked[span, LANES:].astype(jnp.bfloat16)

    rank_col = jnp.sum((same & (lane < sub)).astype(jnp.float32), axis=1, keepdims=True)
    rank_col = jnp.broadcast_to(rank_col, square).astype(jnp.int32)
    half = cap // 2
    place = relative(owner_col) * half + rank_col
    lo_ref[...] = ((rank_col < half) & (place == lane)).astype(jnp.float32).astype(jnp.bfloat16)
    hi_ref[...] = ((rank_col >= half) & (place - half == lane)).astype(jnp.float32).astype(jnp.bfloat16)


def project(row_refs, gain_ref, w_ref, b_ref, qkv_ref, live_ref, block):
    width = gain_ref.shape[1]
    cols = w_ref.shape[1]
    pad = qkv_ref.shape[2] // 3
    first_col = (iota((8, width), 1) == 0).astype(jnp.float32).astype(jnp.bfloat16)
    for r in range(SEC):
        rows = jnp.concatenate([ref[...].reshape(-1, width) for ref in row_refs[2 * r : 2 * r + 2]], axis=0)
        live_ref[block + r] = dot_t(first_col, rows)
        wide = rows.astype(jnp.float32)
        mean_sq = jnp.mean(wide * wide, axis=-1, keepdims=True)
        normed = (wide * lax.rsqrt(mean_sq + NORM_EPS) * gain_ref[...]).astype(jnp.bfloat16)
        for part in range(3):
            out = dot_t(normed, w_ref[part]) + b_ref[part : part + 1, :].astype(jnp.float32)
            qkv_ref[block + r, :, part * pad : part * pad + cols] = out.astype(jnp.bfloat16)
            qkv_ref[block + r, :, part * pad + cols : (part + 1) * pad] = jnp.zeros(
                (rows.shape[0], pad - cols), jnp.bfloat16
            )


def project_kernel(*refs):
    row_refs, (gain_ref, w_ref, b_ref, qkv_ref, live_ref) = refs[:4], refs[4:]
    project(row_refs, gain_ref, w_ref, b_ref, qkv_ref, live_ref, 0)


def attend_kernel(pos_ref, req_ref, *refs):
    early = PLANES - 1
    qkv_in, live_in, row_refs = refs[:early], refs[early : 2 * early], refs[2 * early : 2 * early + 4]
    gain_ref, w_ref, b_ref = refs[2 * early + 4 : 2 * early + 7]
    out_refs = refs[2 * early + 7 : 2 * early + 7 + LINES]
    qkv, live, sems = refs[2 * early + 7 + LINES :]
    copies = []
    for j in range(early):
        span = pl.ds(SEC * j, SEC)
        copies.append(pltpu.make_async_copy(qkv_in[j], qkv.at[span], sems.at[0, j]))
        copies.append(pltpu.make_async_copy(live_in[j], live.at[span], sems.at[1, j]))
    for copy in copies:
        copy.start()
    project(row_refs, gain_ref, w_ref, b_ref, qkv, live, SEC * early)
    for copy in copies:
        copy.wait()

    dev, sec = pos_ref[0], pos_ref[1]
    pad = qkv.shape[2] // 3
    cols = w_ref.shape[1]
    group = qkv.shape[1] // LINES
    half = group // 2
    most = BLOCKS // 2

    def block_of(position):
        return ((position & (PLANES - 1)) ^ dev) * SEC + ((position // PLANES) ^ sec)

    for r in range(SEC):

        @pl.loop(0, PLANES)
        def _(j):
            block = SEC * j + r
            own = req_ref[0, (sec ^ r) * PLANES + (dev ^ j)]
            first, count = jnp.int32(0), jnp.int32(0)
            for s in range(BLOCKS):
                first = first + (req_ref[0, s] < own).astype(jnp.int32)
                count = count + (req_ref[0, s] == own).astype(jnp.int32)
            keys, biases = [], []
            for i in range(most):
                key = block_of(first + jnp.minimum(i, count - 1))
                shut = jnp.where(i < count, 0.0, NEG)
                keys.append(key)
                biases.append(jnp.where(live[key][:1] < EMPTY / 2, shut, NEG))
            tile = [None] * (pad // LANES)
            for head in range(cols // HD):
                lo, hi = tiles_of(head)
                mask = head_mask(head)
                query = qkv[block, :, lo * LANES : hi * LANES]
                query = jnp.where(mask, query, jnp.zeros((), jnp.bfloat16))
                scores = []
                for key, bias in zip(keys, biases):
                    k_rows = qkv[key, :, pad + lo * LANES : pad + hi * LANES]
                    scores.append(dot_t(query, k_rows) * HD ** (-0.5) + bias)
                top = functools.reduce(jnp.maximum, scores)
                top = jnp.max(top, axis=1, keepdims=True)
                expo = [jnp.exp(s - top) for s in scores]
                total = jnp.sum(functools.reduce(jnp.add, expo), axis=1, keepdims=True)
                inverse = 1.0 / total
                mixed = None
                for key, e in zip(keys, expo):
                    v_rows = qkv[key, :, 2 * pad + lo * LANES : 2 * pad + hi * LANES]
                    term = dot_n((e * inverse).astype(jnp.bfloat16), v_rows)
                    mixed = term if mixed is None else mixed + term
                for t in range(lo, hi):
                    part = slice((t - lo) * LANES, (t - lo + 1) * LANES)
                    piece = jnp.where(mask[:, part], mixed[:, part], 0.0)
                    tile[t] = piece if tile[t] is None else tile[t] + piece
            plain = jnp.concatenate(tile, axis=1)
            shift = cols % LANES
            moved = pltpu.roll(plain, shift, 1)
            whole = cols // LANES
            for g in range(LINES):
                m = LINE_ORDER[r][g]
                up = plain[g * group : g * group + half]
                down = moved[g * group + half : (g + 1) * group]
                out = out_refs[m]
                out[block, :, : whole * LANES] = up[:, : whole * LANES].astype(jnp.bfloat16)
                seam = up[:, whole * LANES :] + down[:, :LANES]
                out[block, :, whole * LANES : (whole + 1) * LANES] = seam.astype(jnp.bfloat16)
                out[block, :, (whole + 1) * LANES :] = down[:, LANES:].astype(jnp.bfloat16)


def finish_kernel(pos_ref, moved_ref, lo_ref, hi_ref, *refs):
    in_refs, out_ref, stack = refs[:BLOCKS], refs[BLOCKS], refs[BLOCKS + 1]
    line = pos_ref[2]
    half, wide = in_refs[0].shape[1:]
    for b in range(BLOCKS):
        for m in range(LINES):
            stack[m, b * half : (b + 1) * half, :] = in_refs[b][m]
    cols = wide // 2
    low = iota((1, wide), 1) < cols
    for pair in range(LINES // 2):
        lo, hi = [], []
        for k in (2 * pair, 2 * pair + 1):
            rows = stack[line ^ k]
            lo.append(dot_n(lo_ref[...], rows))
            hi.append(dot_n(hi_ref[...], rows))
        back = jnp.where(low, lo[0], hi[1]) + pltpu.roll(jnp.where(low, lo[1], hi[0]), cols, 1)
        span = slice(pair * wide, (pair + 1) * wide)
        out_ref[:, span] = (moved_ref[:, span].astype(jnp.float32) + back).astype(jnp.bfloat16)


def smem():
    return pl.BlockSpec(memory_space=pltpu.SMEM)


def vmem():
    return pl.BlockSpec(memory_space=pltpu.VMEM)


def kept(shape, dtype=jnp.bfloat16):
    return jax.ShapeDtypeStruct(shape, dtype)


def to_block(x, b):
    j, r = b // SEC, b % SEC
    pairs = [
        (s * PLANES + d, (s ^ r) * PLANES + (d ^ j)) for s in range(SEC) for d in range(PLANES)
    ]
    return lax.ppermute(x, ("sec", "dev"), pairs)


def to_line(x, m):
    return lax.ppermute(x, "sp", [(i, i ^ m) for i in range(LINES)])


def shards(
    patch_qkv, patch_state, window_index, patch_owner, source_request, norm_gain, w_qkv, b_qkv
):
    rows, _, width = patch_qkv.shape
    cap = 2 * rows // BLOCKS
    cols = w_qkv.shape[2]
    pad = -(-cols // LANES) * LANES
    half = cap // 2
    block_rows = LINES * cap
    pos = jnp.stack([lax.axis_index("dev"), lax.axis_index("sec"), lax.axis_index("sp")]).astype(jnp.int32)

    moved, lo, hi, *sent = pl.pallas_call(
        window_kernel,
        out_shape=[kept((rows, width)), kept((rows, rows)), kept((rows, rows))]
        + [kept((cap, width))] * BLOCKS,
        in_specs=[smem()] + [vmem()] * 4,
        out_specs=[vmem()] * (3 + BLOCKS),
        name="window",
    )(pos, jnp.transpose(patch_qkv, (1, 0, 2)), patch_state, window_index, patch_owner.reshape(1, rows))

    came = [sent[0] if b == 0 else to_block(sent[b], b) for b in range(BLOCKS)]
    gathered = []
    for j in range(PLANES):
        a, b = came[SEC * j][None], came[SEC * j + 1][None]
        a2 = jnp.concatenate([a, to_line(a, 1)], axis=0)
        b2 = jnp.concatenate([b, to_line(b, 2)], axis=0)
        gathered.append([a2, to_line(a2, 2), b2, to_line(b2, 1)])

    gain = norm_gain.reshape(1, width)
    weights = jnp.transpose(w_qkv, (1, 2, 0))
    qkv_shape, live_shape = (SEC, block_rows, 3 * pad), (SEC, 8, block_rows)
    projected = []
    for j in range(PLANES - 1):
        projected.append(
            pl.pallas_call(
                project_kernel,
                out_shape=[kept(qkv_shape), kept(live_shape, jnp.float32)],
                in_specs=[vmem()] * 7,
                out_specs=[vmem()] * 2,
                name="project",
                cost_estimate=pl.CostEstimate(
                    flops=2 * SEC * block_rows * width * 3 * cols, bytes_accessed=4 << 20, transcendentals=0
                ),
            )(*gathered[j], gain, weights, b_qkv)
        )
    mixed = pl.pallas_call(
        attend_kernel,
        out_shape=[kept((BLOCKS, half, 2 * cols))] * LINES,
        in_specs=[smem()] * 2 + [pl.BlockSpec(memory_space=pl.ANY)] * (2 * PLANES - 2) + [vmem()] * 7,
        out_specs=[vmem()] * LINES,
        scratch_shapes=[
            pltpu.VMEM((BLOCKS, block_rows, 3 * pad), jnp.bfloat16),
            pltpu.VMEM((BLOCKS, 8, block_rows), jnp.float32),
            pltpu.SemaphoreType.DMA((2, PLANES - 1)),
        ],
        name="attend",
    )(
        pos,
        source_request,
        *[p[0] for p in projected],
        *[p[1] for p in projected],
        *gathered[-1],
        gain,
        weights,
        b_qkv,
    )

    lines = [mixed[0]] + [to_line(mixed[m], m) for m in range(1, LINES)]
    back = []
    for b in range(BLOCKS):
        joined = jnp.stack([line[b] for line in lines])
        back.append(joined if b == 0 else to_block(joined, b))

    return pl.pallas_call(
        finish_kernel,
        out_shape=kept((rows, width)),
        in_specs=[smem()] + [vmem()] * (3 + BLOCKS),
        out_specs=vmem(),
        scratch_shapes=[pltpu.VMEM((LINES, BLOCKS * half, 2 * cols), jnp.bfloat16)],
        name="finish",
    )(pos, moved, lo, hi, *back)


def solution(mesh):
    in_specs = (
        P(("sec", "sp", "dev"), None, None),
        P(("sec", "sp", "dev"), None),
        P(("sec", "sp", "dev"), None),
        P(("sec", "sp", "dev"), None),
        P(("sec", "dev"), None),
        P(),
        P(None, None, "sp"),
        P(None, "sp"),
    )
    out_specs = P(("sec", "sp", "dev"), None)
    sizes = (mesh.shape["sec"], mesh.shape["sp"], mesh.shape["dev"])
    body = shards if sizes == (SEC, LINES, PLANES) else shards_general
    return jax.shard_map(body, mesh=mesh, in_specs=in_specs, out_specs=out_specs, check_vma=False)
```

```python
import functools

import jax
import jax.numpy as jnp
from jax import lax
from jax.experimental import pallas as pl
from jax.experimental.pallas import tpu as pltpu
from jax.sharding import PartitionSpec as P


HD = 80
WIN = 64
NORM_EPS = 1e-06
NEG = -1e30
EMPTY = 2.0**60
LANES = 128
WINDOW_MIB = 60
RATE = HD ** (-0.5) * 1.4426950408889634


def normalize(rows_in, gain_row):
    rows_in = rows_in.astype(jnp.float32)
    mean_sq = jnp.mean(rows_in * rows_in, axis=-1, keepdims=True)
    return (rows_in * lax.rsqrt(mean_sq + NORM_EPS) * gain_row).astype(jnp.bfloat16)


def softmax_rows(scores):
    row_max = jnp.max(scores, axis=-1, keepdims=True)
    expo_vals = jnp.exp(scores - row_max)
    return (expo_vals / jnp.sum(expo_vals, axis=-1, keepdims=True)).astype(jnp.bfloat16)


def window_attend(qkv_rows, order_ids, head_size, window_span):
    num_rows = qkv_rows.shape[0]
    row_width = qkv_rows.shape[2]
    head_count = row_width // head_size
    ordered = jnp.take(qkv_rows, order_ids, axis=0)
    ordered = ordered.reshape(num_rows // window_span, window_span, 3, head_count, head_size)
    scores = jnp.einsum(
        "wqhd,wkhd->whqk", ordered[:, :, 0], ordered[:, :, 1], preferred_element_type=jnp.float32
    ) * head_size ** (-0.5)
    weights = softmax_rows(scores)
    mixed = jnp.einsum(
        "whqk,wkhd->wqhd", weights, ordered[:, :, 2], preferred_element_type=jnp.float32
    )
    mixed = mixed.reshape(num_rows, row_width).astype(jnp.bfloat16)
    return jnp.zeros((num_rows, row_width), jnp.bfloat16).at[order_ids].set(mixed)


def owner_attend(query, keys_all, values_all, request, live_keys, head_size):
    group_size, head_count, _ = query.shape
    q_block = 512
    scale = head_size ** (-0.5)
    open_keys = live_keys > 0

    def one_block(block_start):
        rows_q = lax.dynamic_slice_in_dim(query, block_start, q_block, 0)
        reqs_q = lax.dynamic_slice_in_dim(request, block_start, q_block, 0)
        scores = jnp.einsum("qhd,khd->hqk", rows_q, keys_all, preferred_element_type=jnp.float32)
        allowed = (reqs_q[:, None] == request[None, :]) & open_keys[None, :]
        scores = jnp.where(allowed[None], scores * scale, NEG)
        weights = softmax_rows(scores)
        mixed = jnp.einsum("hqk,khd->qhd", weights, values_all, preferred_element_type=jnp.float32)
        return mixed.astype(jnp.bfloat16)

    starts = jnp.arange(group_size // q_block, dtype=jnp.int32) * q_block
    blocks = lax.map(one_block, starts)
    return blocks.reshape(group_size, head_count * head_size)


def shards_general(
    patch_qkv, patch_state, window_index, patch_owner, source_request, norm_gain, w_qkv, b_qkv
):
    num_rows = patch_qkv.shape[0]
    row_width = patch_qkv.shape[2]
    sections = lax.axis_size("sec")
    groups = lax.axis_size("sp")
    members = lax.axis_size("dev")
    owners = sections * members
    capacity = max(2, 2 * num_rows // owners)
    local_width = w_qkv.shape[2]
    local_heads = local_width // HD
    window_out = lax.optimization_barrier(window_attend(patch_qkv, window_index[0], HD, WIN))
    moved = (patch_state.astype(jnp.float32) + window_out.astype(jnp.float32)).astype(jnp.bfloat16)
    owner_id = patch_owner[:, 0]
    owner_hits = (owner_id[:, None] == jnp.arange(owners, dtype=jnp.int32)[None, :]).astype(
        jnp.int32
    )
    slot_rank = jnp.sum((jnp.cumsum(owner_hits, axis=0) - 1) * owner_hits, axis=1)
    slot_id = owner_id * capacity + slot_rank
    picker = (jnp.arange(owners * capacity, dtype=jnp.int32)[:, None] == slot_id[None, :]).astype(
        jnp.bfloat16
    )
    outgoing = jnp.dot(picker, moved, preferred_element_type=jnp.float32).astype(jnp.bfloat16)
    outgoing = outgoing.reshape(owners, capacity, row_width)
    filled = jnp.max(picker, axis=1).reshape(owners, capacity)
    incoming, arrived = (
        lax.all_to_all(outgoing, ("sec", "dev"), split_axis=0, concat_axis=0, tiled=True),
        lax.all_to_all(filled, ("sec", "dev"), split_axis=0, concat_axis=0, tiled=True),
    )
    group_size = owners * groups * capacity
    rows_all, live_all = (
        lax.all_gather(incoming, "sp", axis=1, tiled=True),
        lax.all_gather(arrived, "sp", axis=1, tiled=True),
    )
    normed = normalize(rows_all.reshape(group_size, row_width), norm_gain)
    projected = jnp.einsum("gf,fch->gch", normed, w_qkv, preferred_element_type=jnp.float32)
    projected = (projected + b_qkv.astype(jnp.float32)).astype(jnp.bfloat16)
    query = projected[:, 0].reshape(group_size, local_heads, HD)
    keys_all = projected[:, 1].reshape(group_size, local_heads, HD)
    values_all = projected[:, 2].reshape(group_size, local_heads, HD)
    request = jnp.repeat(source_request[0], groups * capacity)
    live_keys = live_all.reshape(group_size)
    mixed = owner_attend(query, keys_all, values_all, request, live_keys, HD)
    pieces = mixed.reshape(owners, groups, capacity, local_width)
    returned = lax.all_to_all(pieces, "sp", split_axis=1, concat_axis=3, tiled=True).reshape(
        owners, capacity, row_width
    )
    result = lax.all_to_all(returned, ("sec", "dev"), split_axis=0, concat_axis=0, tiled=True)
    result = result.reshape(owners * capacity, row_width)
    back_rows = jnp.einsum("sp,sw->pw", picker, result, preferred_element_type=jnp.float32)
    return (moved.astype(jnp.float32) + back_rows).astype(jnp.bfloat16)


SEC, LINES, PLANES = 2, 4, 4
BLOCKS = SEC * PLANES
GROUPS = ((0,), (1, 2), (3,))


def dot_t(a, b):
    return lax.dot_general(a, b, (((1,), (1,)), ((), ())), preferred_element_type=jnp.float32)


def dot_n(a, b):
    return lax.dot_general(a, b, (((1,), (0,)), ((), ())), preferred_element_type=jnp.float32)


def iota(shape, dim):
    return lax.broadcasted_iota(jnp.int32, shape, dim)


def tiles_of(head):
    first, last = head * HD // LANES, (head * HD + HD - 1) // LANES
    return first, last + 1


def head_mask(head):
    first, end = tiles_of(head)
    lane = iota((1, (end - first) * LANES), 1) + first * LANES
    return (lane >= head * HD) & (lane < head * HD + HD)


def window_kernel(
    qkv_hbm, state_hbm, order_ref, owner_ref, moved_ref, lo_ref, hi_ref, *refs
):
    out_refs = refs[:BLOCKS]
    qkv_ref, state_ref, mixed_ref, value_ref, score_ref, pick_ref, mark_ref, sems = refs[BLOCKS:]
    rows, width = state_ref.shape
    heads = width // HD
    cap = out_refs[0].shape[0]
    dev, sec = lax.axis_index("dev"), lax.axis_index("sec")
    square = (rows, rows)
    sub, lane = iota(square, 0), iota(square, 1)

    parts = 2
    span = width // parts
    loads = []
    for p in range(parts):
        cols = pl.ds(p * span, span)
        for n, kinds in enumerate((pl.ds(0, 2), pl.ds(2, 1))):
            src, dst = qkv_hbm.at[kinds, :, cols], qkv_ref.at[kinds, :, cols]
            loads.append(pltpu.make_async_copy(src, dst, sems.at[2 * p + n]))
    loads.append(pltpu.make_async_copy(state_hbm, state_ref, sems.at[2 * parts]))
    for load in loads:
        load.start()

    owner_row = jnp.broadcast_to(owner_ref[...], square).astype(jnp.float32)
    owner_col = owner_row.T
    same = owner_row == owner_col

    def relative(owner):
        owner = owner.astype(jnp.int32)
        return ((owner & (PLANES - 1)) ^ dev) * SEC + ((owner // PLANES) ^ sec)

    rank_row = jnp.sum((same & (sub < lane)).astype(jnp.float32), axis=0, keepdims=True)
    slot_row = relative(owner_row[:1]) * cap + rank_row.astype(jnp.int32)
    picker = iota((BLOCKS * cap, rows), 0) == jnp.broadcast_to(slot_row, (BLOCKS * cap, rows))
    picker = picker.astype(jnp.float32)
    filled = jnp.sum(picker, axis=1, keepdims=True)
    pick_ref[...] = picker.astype(jnp.bfloat16)
    mark_ref[...] = jnp.where((filled == 0.0) & (iota((BLOCKS * cap, LANES), 1) == 0), EMPTY, 0.0)
    rank_col = jnp.sum((same & (lane < sub)).astype(jnp.float32), axis=1, keepdims=True)
    rank_col = jnp.broadcast_to(rank_col, square).astype(jnp.int32)
    half = cap // 2
    place = relative(owner_col) * half + rank_col
    lo_ref[...] = ((rank_col < half) & (place == lane)).astype(jnp.float32).astype(jnp.bfloat16)
    hi_ref[...] = ((rank_col >= half) & (place - half == lane)).astype(jnp.float32).astype(jnp.bfloat16)

    hit = (jnp.broadcast_to(order_ref[...], square) == sub) & (lane < WIN)
    in_first = jnp.sum(hit.astype(jnp.float32), axis=1, keepdims=True)
    in_first = jnp.broadcast_to(in_first, square)
    bias = jnp.where(in_first == in_first.T, 0.0, NEG)

    for p in range(parts):
        group = range(p * heads // parts, (p + 1) * heads // parts)
        loads[2 * p].wait()
        tops, sums = {}, {}
        for head in group:
            first, end = tiles_of(head)
            cols = slice(first * LANES, end * LANES)
            query = jnp.where(head_mask(head), qkv_ref[0, :, cols], jnp.zeros((), jnp.bfloat16))
            score_ref[head] = dot_t(qkv_ref[1, :, cols], query) * RATE + bias
        loads[2 * p + 1].wait()
        for t in range(p * span // LANES, (p + 1) * span // LANES):
            cols = slice(t * LANES, (t + 1) * LANES)
            value_ref[cols, :] = qkv_ref[2, :, cols].T
        for head in group:
            tops[head] = jnp.max(score_ref[head], axis=0, keepdims=True)
        for head in group:
            expo = jnp.exp2(score_ref[head] - tops[head])
            score_ref[head] = expo
            sums[head] = jnp.sum(expo, axis=0, keepdims=True)
        for head in group:
            weights = (score_ref[head] * (1.0 / sums[head])).astype(jnp.bfloat16)
            cols = slice(head * HD, (head + 1) * HD)
            mixed_ref[cols, :] = dot_n(value_ref[cols, :], weights).astype(jnp.bfloat16)
    loads[2 * parts].wait()
    for t in range(width // LANES):
        cols = slice(t * LANES, (t + 1) * LANES)
        window_out = mixed_ref[cols, :].T.astype(jnp.float32)
        moved_ref[:, cols] = (state_ref[:, cols].astype(jnp.float32) + window_out).astype(jnp.bfloat16)

    picked = dot_n(pick_ref[...], moved_ref[...])
    for b in range(BLOCKS):
        span = slice(b * cap, (b + 1) * cap)
        out_refs[b][:, :LANES] = (picked[span, :LANES] + mark_ref[span, :]).astype(jnp.bfloat16)
        out_refs[b][:, LANES:] = picked[span, LANES:].astype(jnp.bfloat16)


def stores(blocks, block_rows, cols):
    heads = cols // HD
    return (
        (blocks, heads, LANES, block_rows),
        (blocks, block_rows, heads * LANES),
        (blocks, cols, block_rows),
    )


def project(pieces, gain_ref, w_ref, b_ref, kb_ref, q_ref, k_ref, v_ref, q_at, at, normed_ref):
    planes, cap = pieces[0].shape[1:3]
    cols = w_ref.shape[1]
    heads = cols // HD
    block_rows = LINES * cap
    spare = (LANES - HD, block_rows)
    tail = (iota(spare, 0) == 0).astype(jnp.float32).astype(jnp.bfloat16)
    columns = []
    for part in (0, 2):
        row = jnp.pad(b_ref[part : part + 1, :].astype(jnp.float32), ((0, 0), (0, -cols % LANES)))
        column = jnp.broadcast_to(row, (LANES, row.shape[1])).T[:cols]
        columns.append(jnp.concatenate([column] * (SEC * block_rows // LANES), axis=1))
    for j in range(planes):
        for r in range(SEC):
            for step in range(2):
                for n in range(2):
                    m = 2 * step + n if r == 0 else 2 * n + step
                    wide = pieces[2 * r + step][n, j].astype(jnp.float32)
                    shut = jnp.where(wide[:, :1] < EMPTY / 2, 0.0, NEG)
                    mean_sq = jnp.mean(wide * wide, axis=-1, keepdims=True)
                    normed = (wide * lax.rsqrt(mean_sq + NORM_EPS) * gain_ref[...]).astype(jnp.bfloat16)
                    normed_ref[(r * LINES + m) * cap : (r * LINES + m + 1) * cap, :] = normed
                    flag = iota((cap, heads * LANES), 1) % LANES == HD
                    b = at + SEC * j + r
                    k_ref[b, m * cap : (m + 1) * cap, :] = jnp.where(flag, shut, 0.0).astype(jnp.bfloat16)
        rows = normed_ref[...]
        q = (dot_t(w_ref[0], rows) + columns[0]).astype(jnp.bfloat16)
        v = (dot_t(w_ref[2], rows) + columns[1]).astype(jnp.bfloat16)
        for r in range(SEC):
            span = slice(r * block_rows, (r + 1) * block_rows)
            v_ref[at + SEC * j + r] = v[:, span]
            for head in range(heads):
                q_ref[q_at + SEC * j + r, head, :HD, :] = q[head * HD : (head + 1) * HD, span]
                q_ref[q_at + SEC * j + r, head, HD:, :] = tail
        for head in range(heads):
            k = dot_t(rows, w_ref[1, head * HD : (head + 1) * HD, :]) + kb_ref[head : head + 1, :]
            k = k.astype(jnp.bfloat16)
            for r in range(SEC):
                span = slice(r * block_rows, (r + 1) * block_rows)
                k_ref[at + SEC * j + r, :, head * LANES : head * LANES + HD] = k[span]


def project_kernel(*refs):
    pieces, (gain_ref, w_ref, b_ref, kb_ref, q_ref, k_ref, v_ref, normed_ref) = refs[:4], refs[4:]
    project(pieces, gain_ref, w_ref, b_ref, kb_ref, q_ref, k_ref, v_ref, 0, 0, normed_ref)


def attend(req_ref, q_ref, k_ref, v_ref, first_block, out_refs, score_ref):
    dev, sec = lax.axis_index("dev"), lax.axis_index("sec")
    heads = q_ref.shape[1]
    cols, block_rows = v_ref.shape[1:]
    group = block_rows // LINES
    half = group // 2
    most = BLOCKS // 2

    def block_of(position):
        return ((position & (PLANES - 1)) ^ dev) * SEC + ((position // PLANES) ^ sec)

    def one(at, keys):
        mixed, tops, sums = [], [], []
        size = len(keys) * block_rows
        for head in range(heads):
            span = slice(head * LANES, (head + 1) * LANES)
            k_rows = jnp.concatenate([k_ref[key, :, span] for key in keys], axis=0)
            score_ref[head, :size, :] = dot_n(k_rows, q_ref[first_block + at, head])
        parts = [slice(i * block_rows, (i + 1) * block_rows) for i in range(len(keys))]
        for head in range(heads):
            blocks = [score_ref[head, part, :] for part in parts]
            tops.append(jnp.max(functools.reduce(jnp.maximum, blocks), axis=0, keepdims=True) * RATE)
        for head in range(heads):
            total = None
            for part in parts:
                expo = jnp.exp2(score_ref[head, part, :] * RATE - tops[head])
                score_ref[head, part, :] = expo
                total = expo if total is None else total + expo
            sums.append(jnp.sum(total, axis=0, keepdims=True))
        for head in range(heads):
            inverse = 1.0 / sums[head]
            weights = [(score_ref[head, part, :] * inverse).astype(jnp.bfloat16) for part in parts]
            weights = jnp.concatenate(weights, axis=0)
            span = slice(head * HD, (head + 1) * HD)
            values = jnp.concatenate([v_ref[key, span, :] for key in keys], axis=1)
            mixed.append(dot_n(values, weights))
        if cols % LANES:
            mixed.append(jnp.zeros((-cols % LANES, block_rows), jnp.float32))
        plain = jnp.concatenate(mixed, axis=0).T
        moved = pltpu.roll(plain, cols % LANES, 1)
        whole = cols // LANES
        for m in range(LINES):
            up = plain[m * group : m * group + half]
            down = moved[m * group + half : (m + 1) * group]
            out = out_refs[m]
            out[at, :, : whole * LANES] = up[:, : whole * LANES].astype(jnp.bfloat16)
            seam = up[:, whole * LANES :] + down[:, :LANES]
            out[at, :, whole * LANES : (whole + 1) * LANES] = seam.astype(jnp.bfloat16)
            out[at, :, (whole + 1) * LANES :] = down[:, LANES:].astype(jnp.bfloat16)

    @pl.loop(0, out_refs[0].shape[0])
    def _(at):
        block = first_block + at
        own = req_ref[0, (sec ^ (block & 1)) * PLANES + (dev ^ (block // 2))]
        first, count = jnp.int32(0), jnp.int32(0)
        for s in range(BLOCKS):
            first = first + (req_ref[0, s] < own).astype(jnp.int32)
            count = count + (req_ref[0, s] == own).astype(jnp.int32)
        keys = []
        for i in range(most):
            key = block_of(jnp.minimum(first + i, BLOCKS - 1))
            keys.append(jnp.where(i < count, key, BLOCKS))

        @pl.when(count <= most // 2)
        def _():
            one(at, keys[: most // 2])

        @pl.when(count > most // 2)
        def _():
            one(at, keys)


def attend_far_kernel(groups, req_ref, *refs):
    early = groups[:-1]
    ready, refs = refs[: 3 * len(early)], refs[3 * len(early) :]
    pieces, shared, refs = refs[:4], refs[4:8], refs[8:]
    out_refs, (q_ref, k_ref, v_ref, normed_ref, score_ref) = refs[:LINES], refs[LINES:]
    last = SEC * groups[-1][0]
    project(pieces, *shared, q_ref, k_ref, v_ref, last, last, normed_ref)
    for i, planes in enumerate(early):
        span = slice(SEC * planes[0], SEC * (planes[-1] + 1))
        for ref, part in zip((q_ref, k_ref, v_ref), ready[3 * i : 3 * i + 3]):
            ref[span] = part[...]
    flag = iota(k_ref.shape[1:], 1) % LANES == HD
    k_ref[BLOCKS] = jnp.where(flag, NEG, 0.0).astype(jnp.bfloat16)
    v_ref[BLOCKS] = jnp.zeros(v_ref.shape[1:], jnp.bfloat16)
    attend(req_ref, q_ref, k_ref, v_ref, BLOCKS // 2, out_refs, score_ref)


def attend_near_kernel(req_ref, q_ref, k_ref, v_ref, *refs):
    attend(req_ref, q_ref, k_ref, v_ref, 0, refs[:LINES], refs[LINES])


def finish_kernel(moved_ref, lo_ref, hi_ref, *refs):
    in_refs, out_ref = refs[:BLOCKS], refs[BLOCKS]
    line = lax.axis_index("sp")
    wide = in_refs[0].shape[2]
    cols = wide // 2
    low = iota((1, wide), 1) < cols
    for pair in range(LINES // 2):
        lo, hi = [], []
        for k in (2 * pair, 2 * pair + 1):
            rows = jnp.concatenate([ref[line ^ k] for ref in in_refs], axis=0)
            lo.append(dot_n(lo_ref[...], rows))
            hi.append(dot_n(hi_ref[...], rows))
        back = jnp.where(low, lo[0], hi[1]) + pltpu.roll(jnp.where(low, lo[1], hi[0]), cols, 1)
        span = slice(pair * wide, (pair + 1) * wide)
        out_ref[:, span] = (moved_ref[:, span].astype(jnp.float32) + back).astype(jnp.bfloat16)


def smem():
    return pl.BlockSpec(memory_space=pltpu.SMEM)


def vmem():
    return pl.BlockSpec(memory_space=pltpu.VMEM)


def room(mib):
    return pltpu.CompilerParams(vmem_limit_bytes=mib << 20)


def kept(shape, dtype=jnp.bfloat16):
    return jax.ShapeDtypeStruct(shape, dtype)


def to_block(x, b):
    j, r = b // SEC, b % SEC
    pairs = [
        (s * PLANES + d, (s ^ r) * PLANES + (d ^ j)) for s in range(SEC) for d in range(PLANES)
    ]
    return lax.ppermute(x, ("sec", "dev"), pairs)


def to_line(x, m):
    return lax.ppermute(x, "sp", [(i, i ^ m) for i in range(LINES)])


def spread(came, planes):
    a = jnp.stack([came[SEC * j] for j in planes])[None]
    b = jnp.stack([came[SEC * j + 1] for j in planes])[None]
    a2 = jnp.concatenate([a, to_line(a, 1)], axis=0)
    b2 = jnp.concatenate([b, to_line(b, 2)], axis=0)
    return [a2, to_line(a2, 2), b2, to_line(b2, 1)]


def shards(*args):
    return shards_here(*args)


def shards_here(
    patch_qkv, patch_state, window_index, patch_owner, source_request, norm_gain, w_qkv, b_qkv
):
    rows, _, width = patch_qkv.shape
    cap = 2 * rows // BLOCKS
    cols = w_qkv.shape[2]
    half = cap // 2
    block_rows = LINES * cap
    heads = cols // HD

    moved, lo, hi, *sent = pl.pallas_call(
        window_kernel,
        out_shape=[kept((rows, width)), kept((rows, rows)), kept((rows, rows))]
        + [kept((cap, width))] * BLOCKS,
        in_specs=[pl.BlockSpec(memory_space=pltpu.HBM)] * 2 + [vmem()] * 2,
        out_specs=[vmem()] * (3 + BLOCKS),
        scratch_shapes=[
            pltpu.VMEM((3, rows, width), jnp.bfloat16),
            pltpu.VMEM((rows, width), jnp.bfloat16),
            pltpu.VMEM((width, rows), jnp.bfloat16),
            pltpu.VMEM((width, rows), jnp.bfloat16),
            pltpu.VMEM((width // HD, rows, rows), jnp.float32),
            pltpu.VMEM((BLOCKS * cap, rows), jnp.bfloat16),
            pltpu.VMEM((BLOCKS * cap, LANES), jnp.float32),
            pltpu.SemaphoreType.DMA((5,)),
        ],
        name="window",
        compiler_params=room(WINDOW_MIB),
    )(jnp.transpose(patch_qkv, (1, 0, 2)), patch_state, window_index, patch_owner.reshape(1, rows))

    came = [sent[0] if b == 0 else to_block(sent[b], b) for b in range(BLOCKS)]
    gathered = [spread(came, planes) for planes in GROUPS]

    key_bias = b_qkv[1].astype(jnp.float32).reshape(heads, HD)
    gain = norm_gain.reshape(1, width)
    shared = (gain, jnp.transpose(w_qkv, (1, 2, 0)), b_qkv, key_bias)

    def projected(pieces, planes):
        return pl.pallas_call(
            project_kernel,
            out_shape=[kept(shape) for shape in stores(SEC * planes, block_rows, cols)],
            in_specs=[vmem()] * 8,
            out_specs=[vmem()] * 3,
            scratch_shapes=[pltpu.VMEM((SEC * block_rows, width), jnp.bfloat16)],
            name="project",
            compiler_params=room(16),
            cost_estimate=pl.CostEstimate(
                flops=2 * SEC * planes * block_rows * width * 4 * cols, bytes_accessed=4 << 20, transcendentals=0
            ),
        )(*pieces, *shared)

    ready = []
    for i, planes in enumerate(GROUPS[:-1]):
        ready += projected(gathered[i], len(planes))
    q_store = stores(BLOCKS, block_rows, cols)[0]
    _, k_store, v_store = stores(BLOCKS + 1, block_rows, cols)
    scores = pltpu.VMEM((heads, BLOCKS // 2 * block_rows, block_rows), jnp.float32)
    *far_mixed, queries, keys, values = pl.pallas_call(
        functools.partial(attend_far_kernel, GROUPS),
        out_shape=[kept((BLOCKS // 2, half, 2 * cols))] * LINES + [kept(q_store), kept(k_store), kept(v_store)],
        in_specs=[smem()] + [vmem()] * (len(ready) + 8),
        out_specs=[vmem()] * (LINES + 3),
        scratch_shapes=[pltpu.VMEM((SEC * block_rows, width), jnp.bfloat16), scores],
        name="attend_far",
        compiler_params=room(20),
    )(source_request, *ready, *gathered[-1], *shared)
    near_mixed = pl.pallas_call(
        attend_near_kernel,
        out_shape=[kept((BLOCKS // 2, half, 2 * cols))] * LINES,
        in_specs=[smem()] + [vmem()] * 3,
        out_specs=[vmem()] * LINES,
        scratch_shapes=[scores],
        name="attend_near",
        compiler_params=room(12),
        cost_estimate=pl.CostEstimate(flops=4 << 30, bytes_accessed=6 << 20, transcendentals=2 << 20),
    )(source_request, queries, keys, values)

    far_lines = [far_mixed[0]] + [to_line(far_mixed[m], m) for m in range(1, LINES)]
    near_lines = [near_mixed[0]] + [to_line(near_mixed[m], m) for m in range(1, LINES)]
    back = []
    for b in range(BLOCKS):
        lines, at = (far_lines, b - BLOCKS // 2) if b >= BLOCKS // 2 else (near_lines, b)
        joined = jnp.stack([line[at] for line in lines])
        back.append(joined if b == 0 else to_block(joined, b))

    return pl.pallas_call(
        finish_kernel,
        out_shape=kept((rows, width)),
        in_specs=[vmem()] * (3 + BLOCKS),
        out_specs=vmem(),
        name="finish",
        compiler_params=room(8),
    )(moved, lo, hi, *back)


def solution(mesh):
    in_specs = (
        P(("sec", "sp", "dev"), None, None),
        P(("sec", "sp", "dev"), None),
        P(("sec", "sp", "dev"), None),
        P(("sec", "sp", "dev"), None),
        P(("sec", "dev"), None),
        P(),
        P(None, None, "sp"),
        P(None, "sp"),
    )
    out_specs = P(("sec", "sp", "dev"), None)
    sizes = (mesh.shape["sec"], mesh.shape["sp"], mesh.shape["dev"])
    special = sizes == (SEC, LINES, PLANES)
    body = shards if special else shards_general
    return jax.shard_map(body, mesh=mesh, in_specs=in_specs, out_specs=out_specs, check_vma=False)
```

```python
import functools

import jax
import jax.numpy as jnp
from jax import lax
from jax.experimental import pallas as pl
from jax.experimental.pallas import tpu as pltpu
from jax.sharding import PartitionSpec as P


HD = 80
WIN = 64
NORM_EPS = 1e-06
NEG = -1e30
EMPTY = 2.0**60
LANES = 128
WINDOW_MIB = 60
RATE = HD ** (-0.5) * 1.4426950408889634


def normalize(rows_in, gain_row):
    rows_in = rows_in.astype(jnp.float32)
    mean_sq = jnp.mean(rows_in * rows_in, axis=-1, keepdims=True)
    return (rows_in * lax.rsqrt(mean_sq + NORM_EPS) * gain_row).astype(jnp.bfloat16)


def softmax_rows(scores):
    row_max = jnp.max(scores, axis=-1, keepdims=True)
    expo_vals = jnp.exp(scores - row_max)
    return (expo_vals / jnp.sum(expo_vals, axis=-1, keepdims=True)).astype(jnp.bfloat16)


def window_attend(qkv_rows, order_ids, head_size, window_span):
    num_rows = qkv_rows.shape[0]
    row_width = qkv_rows.shape[2]
    head_count = row_width // head_size
    ordered = jnp.take(qkv_rows, order_ids, axis=0)
    ordered = ordered.reshape(num_rows // window_span, window_span, 3, head_count, head_size)
    scores = jnp.einsum(
        "wqhd,wkhd->whqk", ordered[:, :, 0], ordered[:, :, 1], preferred_element_type=jnp.float32
    ) * head_size ** (-0.5)
    weights = softmax_rows(scores)
    mixed = jnp.einsum(
        "whqk,wkhd->wqhd", weights, ordered[:, :, 2], preferred_element_type=jnp.float32
    )
    mixed = mixed.reshape(num_rows, row_width).astype(jnp.bfloat16)
    return jnp.zeros((num_rows, row_width), jnp.bfloat16).at[order_ids].set(mixed)


def owner_attend(query, keys_all, values_all, request, live_keys, head_size):
    group_size, head_count, _ = query.shape
    q_block = 512
    scale = head_size ** (-0.5)
    open_keys = live_keys > 0

    def one_block(block_start):
        rows_q = lax.dynamic_slice_in_dim(query, block_start, q_block, 0)
        reqs_q = lax.dynamic_slice_in_dim(request, block_start, q_block, 0)
        scores = jnp.einsum("qhd,khd->hqk", rows_q, keys_all, preferred_element_type=jnp.float32)
        allowed = (reqs_q[:, None] == request[None, :]) & open_keys[None, :]
        scores = jnp.where(allowed[None], scores * scale, NEG)
        weights = softmax_rows(scores)
        mixed = jnp.einsum("hqk,khd->qhd", weights, values_all, preferred_element_type=jnp.float32)
        return mixed.astype(jnp.bfloat16)

    starts = jnp.arange(group_size // q_block, dtype=jnp.int32) * q_block
    blocks = lax.map(one_block, starts)
    return blocks.reshape(group_size, head_count * head_size)


def shards_general(
    patch_qkv, patch_state, window_index, patch_owner, source_request, norm_gain, w_qkv, b_qkv
):
    num_rows = patch_qkv.shape[0]
    row_width = patch_qkv.shape[2]
    sections = lax.axis_size("sec")
    groups = lax.axis_size("sp")
    members = lax.axis_size("dev")
    owners = sections * members
    capacity = max(2, 2 * num_rows // owners)
    local_width = w_qkv.shape[2]
    local_heads = local_width // HD
    window_out = lax.optimization_barrier(window_attend(patch_qkv, window_index[0], HD, WIN))
    moved = (patch_state.astype(jnp.float32) + window_out.astype(jnp.float32)).astype(jnp.bfloat16)
    owner_id = patch_owner[:, 0]
    owner_hits = (owner_id[:, None] == jnp.arange(owners, dtype=jnp.int32)[None, :]).astype(
        jnp.int32
    )
    slot_rank = jnp.sum((jnp.cumsum(owner_hits, axis=0) - 1) * owner_hits, axis=1)
    slot_id = owner_id * capacity + slot_rank
    picker = (jnp.arange(owners * capacity, dtype=jnp.int32)[:, None] == slot_id[None, :]).astype(
        jnp.bfloat16
    )
    outgoing = jnp.dot(picker, moved, preferred_element_type=jnp.float32).astype(jnp.bfloat16)
    outgoing = outgoing.reshape(owners, capacity, row_width)
    filled = jnp.max(picker, axis=1).reshape(owners, capacity)
    incoming, arrived = (
        lax.all_to_all(outgoing, ("sec", "dev"), split_axis=0, concat_axis=0, tiled=True),
        lax.all_to_all(filled, ("sec", "dev"), split_axis=0, concat_axis=0, tiled=True),
    )
    group_size = owners * groups * capacity
    rows_all, live_all = (
        lax.all_gather(incoming, "sp", axis=1, tiled=True),
        lax.all_gather(arrived, "sp", axis=1, tiled=True),
    )
    normed = normalize(rows_all.reshape(group_size, row_width), norm_gain)
    projected = jnp.einsum("gf,fch->gch", normed, w_qkv, preferred_element_type=jnp.float32)
    projected = (projected + b_qkv.astype(jnp.float32)).astype(jnp.bfloat16)
    query = projected[:, 0].reshape(group_size, local_heads, HD)
    keys_all = projected[:, 1].reshape(group_size, local_heads, HD)
    values_all = projected[:, 2].reshape(group_size, local_heads, HD)
    request = jnp.repeat(source_request[0], groups * capacity)
    live_keys = live_all.reshape(group_size)
    mixed = owner_attend(query, keys_all, values_all, request, live_keys, HD)
    pieces = mixed.reshape(owners, groups, capacity, local_width)
    returned = lax.all_to_all(pieces, "sp", split_axis=1, concat_axis=3, tiled=True).reshape(
        owners, capacity, row_width
    )
    result = lax.all_to_all(returned, ("sec", "dev"), split_axis=0, concat_axis=0, tiled=True)
    result = result.reshape(owners * capacity, row_width)
    back_rows = jnp.einsum("sp,sw->pw", picker, result, preferred_element_type=jnp.float32)
    return (moved.astype(jnp.float32) + back_rows).astype(jnp.bfloat16)


SEC, LINES, PLANES = 2, 4, 4
BLOCKS = SEC * PLANES
GROUPS = ((0,), (2,), (1, 3))


def dot_t(a, b):
    return lax.dot_general(a, b, (((1,), (1,)), ((), ())), preferred_element_type=jnp.float32)


def dot_n(a, b):
    return lax.dot_general(a, b, (((1,), (0,)), ((), ())), preferred_element_type=jnp.float32)


def iota(shape, dim):
    return lax.broadcasted_iota(jnp.int32, shape, dim)


def tiles_of(head):
    first, last = head * HD // LANES, (head * HD + HD - 1) // LANES
    return first, last + 1


def head_mask(head):
    first, end = tiles_of(head)
    lane = iota((1, (end - first) * LANES), 1) + first * LANES
    return (lane >= head * HD) & (lane < head * HD + HD)


def window_kernel(
    qkv_hbm, state_hbm, order_ref, owner_ref, moved_ref, lo_ref, hi_ref, *refs
):
    out_refs = refs[:BLOCKS]
    qkv_ref, state_ref, mixed_ref, value_ref, score_ref, pick_ref, mark_ref, sems = refs[BLOCKS:]
    rows, width = state_ref.shape
    heads = width // HD
    cap = out_refs[0].shape[0]
    dev, sec = lax.axis_index("dev"), lax.axis_index("sec")
    square = (rows, rows)
    sub, lane = iota(square, 0), iota(square, 1)

    parts = 2
    span = width // parts
    loads = []
    for p in range(parts):
        cols = pl.ds(p * span, span)
        for n, kinds in enumerate((pl.ds(0, 2), pl.ds(2, 1))):
            src, dst = qkv_hbm.at[kinds, :, cols], qkv_ref.at[kinds, :, cols]
            loads.append(pltpu.make_async_copy(src, dst, sems.at[2 * p + n]))
    loads.append(pltpu.make_async_copy(state_hbm, state_ref, sems.at[2 * parts]))
    for load in loads:
        load.start()

    owner_row = jnp.broadcast_to(owner_ref[...], square).astype(jnp.float32)
    owner_col = owner_row.T
    same = owner_row == owner_col

    def relative(owner):
        owner = owner.astype(jnp.int32)
        return ((owner & (PLANES - 1)) ^ dev) * SEC + ((owner // PLANES) ^ sec)

    rank_row = jnp.sum((same & (sub < lane)).astype(jnp.float32), axis=0, keepdims=True)
    slot_row = relative(owner_row[:1]) * cap + rank_row.astype(jnp.int32)
    picker = iota((BLOCKS * cap, rows), 0) == jnp.broadcast_to(slot_row, (BLOCKS * cap, rows))
    picker = picker.astype(jnp.float32)
    filled = jnp.sum(picker, axis=1, keepdims=True)
    pick_ref[...] = picker.astype(jnp.bfloat16)
    mark_ref[...] = jnp.where((filled == 0.0) & (iota((BLOCKS * cap, LANES), 1) == 0), EMPTY, 0.0)
    rank_col = jnp.sum((same & (lane < sub)).astype(jnp.float32), axis=1, keepdims=True)
    rank_col = jnp.broadcast_to(rank_col, square).astype(jnp.int32)
    half = cap // 2
    place = relative(owner_col) * half + rank_col
    lo_ref[...] = ((rank_col < half) & (place == lane)).astype(jnp.float32).astype(jnp.bfloat16)
    hi_ref[...] = ((rank_col >= half) & (place - half == lane)).astype(jnp.float32).astype(jnp.bfloat16)

    hit = (jnp.broadcast_to(order_ref[...], square) == sub) & (lane < WIN)
    in_first = jnp.sum(hit.astype(jnp.float32), axis=1, keepdims=True)
    in_first = jnp.broadcast_to(in_first, square)
    bias = jnp.where(in_first == in_first.T, 0.0, NEG)

    for p in range(parts):
        group = range(p * heads // parts, (p + 1) * heads // parts)
        loads[2 * p].wait()
        tops, sums = {}, {}
        for head in group:
            first, end = tiles_of(head)
            cols = slice(first * LANES, end * LANES)
            query = jnp.where(head_mask(head), qkv_ref[0, :, cols], jnp.zeros((), jnp.bfloat16))
            score_ref[head] = dot_t(qkv_ref[1, :, cols], query) * RATE + bias
        loads[2 * p + 1].wait()
        for t in range(p * span // LANES, (p + 1) * span // LANES):
            cols = slice(t * LANES, (t + 1) * LANES)
            value_ref[cols, :] = qkv_ref[2, :, cols].T
        for head in group:
            tops[head] = jnp.max(score_ref[head], axis=0, keepdims=True)
        for head in group:
            expo = jnp.exp2(score_ref[head] - tops[head])
            score_ref[head] = expo
            sums[head] = jnp.sum(expo, axis=0, keepdims=True)
        for head in group:
            weights = (score_ref[head] * (1.0 / sums[head])).astype(jnp.bfloat16)
            cols = slice(head * HD, (head + 1) * HD)
            mixed_ref[cols, :] = dot_n(value_ref[cols, :], weights).astype(jnp.bfloat16)
    loads[2 * parts].wait()
    for t in range(width // LANES):
        cols = slice(t * LANES, (t + 1) * LANES)
        window_out = mixed_ref[cols, :].T.astype(jnp.float32)
        moved_ref[:, cols] = (state_ref[:, cols].astype(jnp.float32) + window_out).astype(jnp.bfloat16)

    picked = dot_n(pick_ref[...], moved_ref[...])
    for b in range(BLOCKS):
        span = slice(b * cap, (b + 1) * cap)
        out_refs[b][:, :LANES] = (picked[span, :LANES] + mark_ref[span, :]).astype(jnp.bfloat16)
        out_refs[b][:, LANES:] = picked[span, LANES:].astype(jnp.bfloat16)


def stores(blocks, block_rows, cols):
    heads = cols // HD
    return (
        (blocks, heads, LANES, block_rows),
        (blocks, block_rows, heads * LANES),
        (blocks, cols, block_rows),
    )


def project(pieces, gain_ref, w_ref, b_ref, kb_ref, q_ref, k_ref, v_ref, starts, normed_ref):
    cap = pieces[0].shape[2]
    cols = w_ref.shape[1]
    heads = cols // HD
    block_rows = LINES * cap
    spare = (LANES - HD, block_rows)
    tail = (iota(spare, 0) == 0).astype(jnp.float32).astype(jnp.bfloat16)
    columns = []
    for part in (0, 2):
        row = jnp.pad(b_ref[part : part + 1, :].astype(jnp.float32), ((0, 0), (0, -cols % LANES)))
        column = jnp.broadcast_to(row, (LANES, row.shape[1])).T[:cols]
        columns.append(jnp.concatenate([column] * (SEC * block_rows // LANES), axis=1))
    for j, at in enumerate(starts):
        for r in range(SEC):
            for step in range(2):
                for n in range(2):
                    m = 2 * step + n if r == 0 else 2 * n + step
                    wide = pieces[2 * r + step][n, j].astype(jnp.float32)
                    shut = jnp.where(wide[:, :1] < EMPTY / 2, 0.0, NEG)
                    mean_sq = jnp.mean(wide * wide, axis=-1, keepdims=True)
                    normed = (wide * lax.rsqrt(mean_sq + NORM_EPS) * gain_ref[...]).astype(jnp.bfloat16)
                    normed_ref[(r * LINES + m) * cap : (r * LINES + m + 1) * cap, :] = normed
                    flag = iota((cap, heads * LANES), 1) % LANES == HD
                    k_ref[at + r, m * cap : (m + 1) * cap, :] = jnp.where(flag, shut, 0.0).astype(jnp.bfloat16)
        rows = normed_ref[...]
        q = (dot_t(w_ref[0], rows) + columns[0]).astype(jnp.bfloat16)
        v = (dot_t(w_ref[2], rows) + columns[1]).astype(jnp.bfloat16)
        for r in range(SEC):
            span = slice(r * block_rows, (r + 1) * block_rows)
            v_ref[at + r] = v[:, span]
            for head in range(heads):
                q_ref[at + r, head, :HD, :] = q[head * HD : (head + 1) * HD, span]
                q_ref[at + r, head, HD:, :] = tail
        for head in range(heads):
            k = dot_t(rows, w_ref[1, head * HD : (head + 1) * HD, :]) + kb_ref[head : head + 1, :]
            k = k.astype(jnp.bfloat16)
            for r in range(SEC):
                span = slice(r * block_rows, (r + 1) * block_rows)
                k_ref[at + r, :, head * LANES : head * LANES + HD] = k[span]


def project_kernel(*refs):
    pieces, (gain_ref, w_ref, b_ref, kb_ref, q_ref, k_ref, v_ref, normed_ref) = refs[:4], refs[4:]
    planes = pieces[0].shape[1]
    starts = range(0, SEC * planes, SEC)
    project(pieces, gain_ref, w_ref, b_ref, kb_ref, q_ref, k_ref, v_ref, starts, normed_ref)


def attend(req_ref, q_ref, k_ref, v_ref, first_block, out_refs, score_ref, mixed_ref):
    dev, sec = lax.axis_index("dev"), lax.axis_index("sec")
    heads = q_ref.shape[1]
    cols, block_rows = v_ref.shape[1:]
    group = block_rows // LINES
    half = group // 2
    most = BLOCKS // 2

    if cols % LANES:
        mixed_ref[cols:, :] = jnp.zeros((-cols % LANES, block_rows), jnp.float32)

    def block_of(position):
        return ((position & (PLANES - 1)) ^ dev) * SEC + ((position // PLANES) ^ sec)

    def one(at, keys):
        mixed, tops, sums = [], [], []
        emit(jnp.maximum(at - 1, 0))
        size = len(keys) * block_rows
        for head in range(heads):
            span = slice(head * LANES, (head + 1) * LANES)
            k_rows = jnp.concatenate([k_ref[key, :, span] for key in keys], axis=0)
            score_ref[head, :size, :] = dot_n(k_rows, q_ref[first_block + at, head])
        parts = [slice(i * block_rows, (i + 1) * block_rows) for i in range(len(keys))]
        for head in range(heads):
            blocks = [score_ref[head, part, :] for part in parts]
            tops.append(jnp.max(functools.reduce(jnp.maximum, blocks), axis=0, keepdims=True) * RATE)
        for head in range(heads):
            total = None
            for part in parts:
                expo = jnp.exp2(score_ref[head, part, :] * RATE - tops[head])
                score_ref[head, part, :] = expo
                total = expo if total is None else total + expo
            sums.append(jnp.sum(total, axis=0, keepdims=True))
        for head in range(heads):
            inverse = 1.0 / sums[head]
            weights = [(score_ref[head, part, :] * inverse).astype(jnp.bfloat16) for part in parts]
            weights = jnp.concatenate(weights, axis=0)
            span = slice(head * HD, (head + 1) * HD)
            values = jnp.concatenate([v_ref[key, span, :] for key in keys], axis=1)
            mixed.append(dot_n(values, weights))
        for head in range(heads):
            mixed_ref[head * HD : (head + 1) * HD, :] = mixed[head]

    def emit(at):
        plain = mixed_ref[...].T
        moved = pltpu.roll(plain, cols % LANES, 1)
        whole = cols // LANES
        for m in range(LINES):
            up = plain[m * group : m * group + half]
            down = moved[m * group + half : (m + 1) * group]
            out = out_refs[m]
            out[at, :, : whole * LANES] = up[:, : whole * LANES].astype(jnp.bfloat16)
            seam = up[:, whole * LANES :] + down[:, :LANES]
            out[at, :, whole * LANES : (whole + 1) * LANES] = seam.astype(jnp.bfloat16)
            out[at, :, (whole + 1) * LANES :] = down[:, LANES:].astype(jnp.bfloat16)

    @pl.loop(0, out_refs[0].shape[0])
    def _(at):
        block = first_block + at
        own = req_ref[0, (sec ^ (block & 1)) * PLANES + (dev ^ (block // 2))]
        first, count = jnp.int32(0), jnp.int32(0)
        for s in range(BLOCKS):
            first = first + (req_ref[0, s] < own).astype(jnp.int32)
            count = count + (req_ref[0, s] == own).astype(jnp.int32)
        keys = []
        for i in range(most):
            key = block_of(jnp.minimum(first + i, BLOCKS - 1))
            keys.append(jnp.where(i < count, key, BLOCKS))

        @pl.when(count <= most // 2)
        def _():
            one(at, keys[: most // 2])

        @pl.when(count > most // 2)
        def _():
            one(at, keys)

    emit(out_refs[0].shape[0] - 1)


def attend_far_kernel(groups, req_ref, *refs):
    early = groups[:-1]
    ready, refs = refs[: 3 * len(early)], refs[3 * len(early) :]
    pieces, shared, refs = refs[:4], refs[4:8], refs[8:]
    out_refs, (q_ref, k_ref, v_ref, normed_ref, score_ref, mixed_ref) = refs[:LINES], refs[LINES:]
    starts = [SEC * j for j in groups[-1]]
    for i, planes in enumerate(early):
        for ref, part in zip((q_ref, k_ref, v_ref), ready[3 * i : 3 * i + 3]):
            for n, j in enumerate(planes):
                ref[SEC * j : SEC * (j + 1)] = part[SEC * n : SEC * (n + 1)]
    flag = iota(k_ref.shape[1:], 1) % LANES == HD
    k_ref[BLOCKS] = jnp.where(flag, NEG, 0.0).astype(jnp.bfloat16)
    v_ref[BLOCKS] = jnp.zeros(v_ref.shape[1:], jnp.bfloat16)
    project(pieces, *shared, q_ref, k_ref, v_ref, starts, normed_ref)
    attend(req_ref, q_ref, k_ref, v_ref, BLOCKS // 2, out_refs, score_ref, mixed_ref)


def attend_near_kernel(req_ref, q_ref, k_ref, v_ref, *refs):
    attend(req_ref, q_ref, k_ref, v_ref, 0, refs[:LINES], *refs[LINES:])


def finish_kernel(moved_ref, lo_ref, hi_ref, *refs):
    in_refs, out_ref = refs[:BLOCKS], refs[BLOCKS]
    line = lax.axis_index("sp")
    wide = in_refs[0].shape[2]
    cols = wide // 2
    low = iota((1, wide), 1) < cols
    for pair in range(LINES // 2):
        lo, hi = [], []
        for k in (2 * pair, 2 * pair + 1):
            rows = jnp.concatenate([ref[line ^ k] for ref in in_refs], axis=0)
            lo.append(dot_n(lo_ref[...], rows))
            hi.append(dot_n(hi_ref[...], rows))
        back = jnp.where(low, lo[0], hi[1]) + pltpu.roll(jnp.where(low, lo[1], hi[0]), cols, 1)
        span = slice(pair * wide, (pair + 1) * wide)
        out_ref[:, span] = (moved_ref[:, span].astype(jnp.float32) + back).astype(jnp.bfloat16)


def smem():
    return pl.BlockSpec(memory_space=pltpu.SMEM)


def vmem():
    return pl.BlockSpec(memory_space=pltpu.VMEM)


def room(mib):
    return pltpu.CompilerParams(vmem_limit_bytes=mib << 20)


def kept(shape, dtype=jnp.bfloat16):
    return jax.ShapeDtypeStruct(shape, dtype)


def to_block(x, b):
    j, r = b // SEC, b % SEC
    pairs = [
        (s * PLANES + d, (s ^ r) * PLANES + (d ^ j)) for s in range(SEC) for d in range(PLANES)
    ]
    return lax.ppermute(x, ("sec", "dev"), pairs)


def to_line(x, m):
    return lax.ppermute(x, "sp", [(i, i ^ m) for i in range(LINES)])


def spread(came, planes):
    a = jnp.stack([came[SEC * j] for j in planes])[None]
    b = jnp.stack([came[SEC * j + 1] for j in planes])[None]
    a2 = jnp.concatenate([a, to_line(a, 1)], axis=0)
    b2 = jnp.concatenate([b, to_line(b, 2)], axis=0)
    return [a2, to_line(a2, 2), b2, to_line(b2, 1)]


def shards(*args):
    return shards_here(*args)


def shards_here(
    patch_qkv, patch_state, window_index, patch_owner, source_request, norm_gain, w_qkv, b_qkv
):
    rows, _, width = patch_qkv.shape
    cap = 2 * rows // BLOCKS
    cols = w_qkv.shape[2]
    half = cap // 2
    block_rows = LINES * cap
    heads = cols // HD

    moved, lo, hi, *sent = pl.pallas_call(
        window_kernel,
        out_shape=[kept((rows, width)), kept((rows, rows)), kept((rows, rows))]
        + [kept((cap, width))] * BLOCKS,
        in_specs=[pl.BlockSpec(memory_space=pltpu.HBM)] * 2 + [vmem()] * 2,
        out_specs=[vmem()] * (3 + BLOCKS),
        scratch_shapes=[
            pltpu.VMEM((3, rows, width), jnp.bfloat16),
            pltpu.VMEM((rows, width), jnp.bfloat16),
            pltpu.VMEM((width, rows), jnp.bfloat16),
            pltpu.VMEM((width, rows), jnp.bfloat16),
            pltpu.VMEM((width // HD, rows, rows), jnp.float32),
            pltpu.VMEM((BLOCKS * cap, rows), jnp.bfloat16),
            pltpu.VMEM((BLOCKS * cap, LANES), jnp.float32),
            pltpu.SemaphoreType.DMA((5,)),
        ],
        name="window",
        compiler_params=room(WINDOW_MIB),
    )(jnp.transpose(patch_qkv, (1, 0, 2)), patch_state, window_index, patch_owner.reshape(1, rows))

    came = [sent[0] if b == 0 else to_block(sent[b], b) for b in range(BLOCKS)]
    gathered = [spread(came, planes) for planes in GROUPS]

    key_bias = b_qkv[1].astype(jnp.float32).reshape(heads, HD)
    gain = norm_gain.reshape(1, width)
    shared = (gain, jnp.transpose(w_qkv, (1, 2, 0)), b_qkv, key_bias)

    def projected(pieces, planes):
        return pl.pallas_call(
            project_kernel,
            out_shape=[kept(shape) for shape in stores(SEC * planes, block_rows, cols)],
            in_specs=[vmem()] * 8,
            out_specs=[vmem()] * 3,
            scratch_shapes=[pltpu.VMEM((SEC * block_rows, width), jnp.bfloat16)],
            name="project",
            compiler_params=room(16),
            cost_estimate=pl.CostEstimate(
                flops=2 * SEC * planes * block_rows * width * 4 * cols, bytes_accessed=4 << 20, transcendentals=0
            ),
        )(*pieces, *shared)

    ready = []
    for i, planes in enumerate(GROUPS[:-1]):
        ready += projected(gathered[i], len(planes))
    q_store = stores(BLOCKS, block_rows, cols)[0]
    _, k_store, v_store = stores(BLOCKS + 1, block_rows, cols)
    scores = pltpu.VMEM((heads, BLOCKS // 2 * block_rows, block_rows), jnp.float32)
    sums = pltpu.VMEM((-(-cols // LANES) * LANES, block_rows), jnp.float32)
    *far_mixed, queries, keys, values = pl.pallas_call(
        functools.partial(attend_far_kernel, GROUPS),
        out_shape=[kept((BLOCKS // 2, half, 2 * cols))] * LINES + [kept(q_store), kept(k_store), kept(v_store)],
        in_specs=[smem()] + [vmem()] * (len(ready) + 8),
        out_specs=[vmem()] * (LINES + 3),
        scratch_shapes=[pltpu.VMEM((SEC * block_rows, width), jnp.bfloat16), scores, sums],
        name="attend_far",
        compiler_params=room(20),
    )(source_request, *ready, *gathered[-1], *shared)
    near_mixed = pl.pallas_call(
        attend_near_kernel,
        out_shape=[kept((BLOCKS // 2, half, 2 * cols))] * LINES,
        in_specs=[smem()] + [vmem()] * 3,
        out_specs=[vmem()] * LINES,
        scratch_shapes=[scores, sums],
        name="attend_near",
        compiler_params=room(12),
        cost_estimate=pl.CostEstimate(flops=4 << 30, bytes_accessed=6 << 20, transcendentals=2 << 20),
    )(source_request, queries, keys, values)

    far_lines = [far_mixed[0]] + [to_line(far_mixed[m], m) for m in range(1, LINES)]
    near_lines = [near_mixed[0]] + [to_line(near_mixed[m], m) for m in range(1, LINES)]
    back = []
    for b in range(BLOCKS):
        lines, at = (far_lines, b - BLOCKS // 2) if b >= BLOCKS // 2 else (near_lines, b)
        joined = jnp.stack([line[at] for line in lines])
        back.append(joined if b == 0 else to_block(joined, b))

    return pl.pallas_call(
        finish_kernel,
        out_shape=kept((rows, width)),
        in_specs=[vmem()] * (3 + BLOCKS),
        out_specs=vmem(),
        name="finish",
        compiler_params=room(8),
    )(moved, lo, hi, *back)


def solution(mesh):
    in_specs = (
        P(("sec", "sp", "dev"), None, None),
        P(("sec", "sp", "dev"), None),
        P(("sec", "sp", "dev"), None),
        P(("sec", "sp", "dev"), None),
        P(("sec", "dev"), None),
        P(),
        P(None, None, "sp"),
        P(None, "sp"),
    )
    out_specs = P(("sec", "sp", "dev"), None)
    sizes = (mesh.shape["sec"], mesh.shape["sp"], mesh.shape["dev"])
    special = sizes == (SEC, LINES, PLANES)
    body = shards if special else shards_general
    return jax.shard_map(body, mesh=mesh, in_specs=in_specs, out_specs=out_specs, check_vma=False)
```
